256 devices in a mesh: context: 64 (over z, x, core), head: 4 (over y).
Axes of the slice: x: 4, y: 4, z: 8, core: 2. Of those that a mesh axis runs over, the one named last changes fastest.
Arguments:
- queries: bfloat16 [32768, 4096], P(('context', 'head')), may hold values from -6 to 6
- key_input: bfloat16 [32768, 4096], P(('context', 'head')), may hold values from -32 to 32
- value_input: bfloat16 [32768, 4096], P(('context', 'head')), may hold values from -32 to 32
- gate_input: bfloat16 [32768, 4096], P(('context', 'head')), may hold values from -6 to 6
- decay_logit: float32 [32768, 32], P(('context', 'head')), may hold values from -5 to 16
- beta_logit: float32 [32768, 32], P(('context', 'head')), may hold values from -9 to 9
- decay_bias: float32 [32], P('head'), may hold values from -16 to -3
- norm_gain: float32 [128], replicated, may hold values from 0.1 to 1.9
- doc_start: int32 [512], P('context'), may hold values from 0 to 1, as said below
Outputs:
- layer_output: bfloat16 [32768, 4096], P(('context', 'head'))
The draws below stay inside these ranges and needn't reach their ends.
Inputs may be any that keep to these rules, and one draw needn't show every extreme that they name: `doc_start`: exactly one of the groups 1 to max(3, 64) holds a 1; apart from it, 1 appears only in the last max(2, 64) groups.
All inputs are finite; a program needn't handle non-finite values.
Results may differ from the reference program's by a relative error of at most 0.013.
Values may be sent and summed in bfloat16 or wider, within the bound.
A program may use at most 192 MiB of HBM per device.

```python
import math
import jax
import jax.numpy as jnp
from jax import lax

HEAD_TOTAL = 32
DK = 128
DV = 128
C = 64
TOK_DEV = 128
STREAM_TOKENS = 32768
CH_DEV = 8
NCHUNK = 512


def rough_sample(base_key, row_count, col_count, shown_shared, shown_top, divisor):
    noise_key, shared_key, column_key, scale_key = jax.random.split(base_key, 4)
    sample = jax.random.normal(noise_key, (row_count, col_count), jnp.float32)
    sample = sample + shown_shared * jax.random.normal(shared_key, (1, col_count), jnp.float32)
    column_scale = jnp.exp(jax.random.uniform(column_key, (1, col_count), jnp.float32, 0.0, math.log(shown_top)))
    row_scale = jnp.exp(jax.random.uniform(scale_key, (row_count, 1), jnp.float32, 0.0, math.log(10.0)))
    return jnp.clip(sample * column_scale * row_scale / divisor, -32.0, 32.0)


def draw_key_input(key, part):
    return rough_sample(jax.random.fold_in(key, 11), STREAM_TOKENS, HEAD_TOTAL * DK, 2.5, 100.0, 64.0).astype(jnp.bfloat16)


def draw_value_input(key, part):
    return rough_sample(jax.random.fold_in(key, 13), STREAM_TOKENS, HEAD_TOTAL * DV, 0.0, 10.0, 8.0).astype(jnp.bfloat16)


def decay_pair(key):
    base_key = jax.random.fold_in(key, 31)
    key_sequence = jax.random.split(base_key, 7)
    fast_count = 4
    is_fast = jax.random.randint(key_sequence[0], (HEAD_TOTAL,), 0, 8) < fast_count
    log_tokens = math.log(STREAM_TOKENS)
    slow_bias = -log_tokens - jax.random.uniform(key_sequence[1], (HEAD_TOTAL,), jnp.float32, 1.0, 2.5)
    fast_bias = jax.random.uniform(key_sequence[2], (HEAD_TOTAL,), jnp.float32, -4.3, -3.2)
    per_head_bias = jnp.where(is_fast, fast_bias, slow_bias)
    blocks = STREAM_TOKENS // TOK_DEV
    offset = jax.random.uniform(key_sequence[3], (blocks, 1, HEAD_TOTAL), jnp.float32, -1.0, 1.0)
    jitter = 0.5 * jax.random.normal(key_sequence[4], (blocks, TOK_DEV, HEAD_TOTAL), jnp.float32)
    logit_matrix = (offset + jitter).reshape(STREAM_TOKENS, HEAD_TOTAL)
    token_positions = jax.random.randint(key_sequence[5], (3,), 0, STREAM_TOKENS)
    spike_mask = jnp.any(jnp.arange(STREAM_TOKENS)[:, None] == token_positions[None, :], axis=1)
    spike_value = -per_head_bias[None, :] - jax.random.uniform(key_sequence[6], (STREAM_TOKENS, HEAD_TOTAL), jnp.float32, 0.3, 1.5)
    logit_matrix = jnp.where(spike_mask[:, None], spike_value, logit_matrix)
    return (per_head_bias, jnp.clip(logit_matrix, -5.0, 16.0))


def draw_decay_logit(key, part):
    return decay_pair(key)[1]


def draw_decay_bias(key, part):
    return decay_pair(key)[0]


def draw_doc_start(key, part):
    first_key, coin_key = jax.random.split(jax.random.fold_in(key, 41))
    head_span = max(3, NCHUNK // 8)
    tail_count = max(2, NCHUNK // 8)
    first_group = jax.random.randint(first_key, (), 1, head_span + 1)
    tail_begin = NCHUNK - tail_count
    coin_bound = max(2, min(4 * CH_DEV, tail_count // 2))
    coins = jax.random.randint(coin_key, (NCHUNK,), 0, coin_bound) == 0
    group_index = jnp.arange(NCHUNK, dtype=jnp.int32)
    flags = jnp.logical_or(group_index == first_group, jnp.logical_and(group_index >= tail_begin, coins))
    return flags.astype(jnp.int32)


def shard_levels(own_key, extent, pieces, smallest, high):
    level, own = 1.0, jax.random.fold_in(own_key, 6)
    for dim, shards_of in pieces:
        steps = jnp.exp(jax.random.uniform(jax.random.fold_in(own, dim), (shards_of,), jnp.float32, smallest / len(pieces), high / len(pieces)))
        level = level * jnp.repeat(steps, extent[dim] // shards_of).reshape([-1 if axis == dim else 1 for axis in range(len(extent))])
    return level


def gaussian(own_key, extent, deviation, most, shards=(), held_as=jnp.bfloat16):
    values = deviation * jax.random.normal(own_key, extent, jnp.float32)
    if shards:
        values = values * shard_levels(own_key, extent, shards, -0.22, 0.18)
    return jnp.clip(values, -most, most).astype(held_as)


def setup_inputs(seed: int = 0) -> dict:
    streams_of = jax.random.split(jax.random.key(seed), 10)
    return {
        "queries": gaussian(streams_of[0], (STREAM_TOKENS, HEAD_TOTAL * DK), 1.0, 6.0, ((0, 256),)),
        "key_input": draw_key_input(jax.random.fold_in(streams_of[9], 71), 0),
        "value_input": draw_value_input(jax.random.fold_in(streams_of[9], 71), 0),
        "gate_input": gaussian(streams_of[3], (STREAM_TOKENS, HEAD_TOTAL * DV), 1.0, 6.0, ((0, 256),)),
        "decay_logit": draw_decay_logit(jax.random.fold_in(streams_of[9], 71), 0),
        "beta_logit": gaussian(streams_of[5], (STREAM_TOKENS, HEAD_TOTAL), 1.5, 9.0, ((0, 256),), jnp.float32),
        "decay_bias": draw_decay_bias(jax.random.fold_in(streams_of[9], 71), 0),
        "norm_gain": jnp.clip(1.0 + 0.18 * jax.random.normal(streams_of[7], (DV,), jnp.float32), 0.1, 1.9),
        "doc_start": draw_doc_start(jax.random.fold_in(streams_of[9], 71), 0),
    }


PRECISE = lax.Precision.HIGHEST

def normalize_keys(raw_keys):
    widened = raw_keys.astype(jnp.float32)
    scaled = widened * lax.rsqrt(lax.optimization_barrier(jnp.sum(widened * widened, axis=-1, keepdims=True)) + 1e-06)
    return scaled.astype(jnp.bfloat16)

def group_step(state_in, inputs):
    query_group, key_group, value_group, decay_group, beta_group, start_flag = inputs
    cum_decay = jnp.cumsum(decay_group, axis=0)
    row_index = lax.broadcasted_iota(jnp.int32, (C, C), 0)
    column_index = lax.broadcasted_iota(jnp.int32, (C, C), 1)
    cum_heads = cum_decay.T
    decay_gap = cum_heads[:, :, None] - cum_heads[:, None, :]
    strict = jnp.exp(jnp.where(row_index > column_index, decay_gap, -jnp.inf))
    inclusive = jnp.exp(jnp.where(row_index >= column_index, decay_gap, -jnp.inf))
    query_wide = query_group.astype(jnp.float32)
    key_wide = key_group.astype(jnp.float32)
    value_wide = value_group.astype(jnp.float32)
    key_gram = jnp.einsum('thd,shd->hts', key_wide, key_wide, precision=PRECISE)
    query_gram = jnp.einsum('thd,shd->hts', query_wide, key_wide, precision=PRECISE)
    lower_part = beta_group.T[:, :, None] * strict * key_gram
    scaled_keys = (beta_group * jnp.exp(cum_decay))[:, :, None] * key_wide
    scaled_values = beta_group[:, :, None] * value_wide
    right_side = jnp.transpose(jnp.concatenate([scaled_keys, scaled_values], axis=-1), (1, 0, 2))
    solved = jax.scipy.linalg.solve_triangular(jnp.eye(C, dtype=jnp.float32) + lower_part, right_side, lower=True, unit_diagonal=True)
    solved_keys = solved[:, :, :DK]
    solved_values = solved[:, :, DK:]
    entering = (1.0 - start_flag.astype(jnp.float32)) * state_in
    pseudo = solved_values - jnp.einsum('htd,hde->hte', solved_keys, entering, precision=PRECISE)
    last_cum = cum_decay[-1]
    back_weight = jnp.exp(last_cum[None, :] - cum_decay)
    back_keys = back_weight[:, :, None] * key_wide
    new_state = jnp.exp(last_cum)[:, None, None] * entering + jnp.einsum('thd,hte->hde', back_keys, pseudo, precision=PRECISE)
    query_mix = inclusive * query_gram
    through = jnp.exp(cum_decay)[:, :, None] * jnp.einsum('thd,hde->the', query_wide, entering, precision=PRECISE)
    core_rows = through + jnp.einsum('hts,hse->the', query_mix, pseudo, precision=PRECISE)
    return (new_state, core_rows)

def gated_norm(core_rows, gate_input, norm_gain):
    row_count = core_rows.shape[0]
    widened = core_rows.astype(jnp.float32).reshape(row_count, -1, norm_gain.shape[0])
    scaled = widened * lax.rsqrt(lax.optimization_barrier(jnp.mean(widened * widened, axis=-1, keepdims=True)) + 1e-06)
    gate_wide = gate_input.astype(jnp.float32).reshape(widened.shape)
    result = scaled * norm_gain * jax.nn.silu(gate_wide)
    return result.reshape(row_count, -1).astype(jnp.bfloat16)

def reference(queries, key_input, value_input, gate_input, decay_logit, beta_logit, decay_bias, norm_gain, doc_start):
    groups = STREAM_TOKENS // C
    log_decay = -jax.nn.softplus(decay_logit + decay_bias[None, :])
    beta_gate = jax.nn.sigmoid(beta_logit)
    normed = normalize_keys(key_input.reshape(STREAM_TOKENS, HEAD_TOTAL, DK))
    inputs = (queries.reshape(groups, C, HEAD_TOTAL, DK), normed.reshape(groups, C, HEAD_TOTAL, DK), value_input.reshape(groups, C, HEAD_TOTAL, DV), log_decay.reshape(groups, C, HEAD_TOTAL), beta_gate.reshape(groups, C, HEAD_TOTAL), doc_start)
    start_state = jnp.zeros((HEAD_TOTAL, DK, DV), jnp.float32)
    cores = lax.scan(group_step, start_state, inputs)[1]
    core_rows = cores.reshape(STREAM_TOKENS, HEAD_TOTAL * DV).astype(jnp.bfloat16)
    core_rows = lax.optimization_barrier(core_rows)
    return gated_norm(core_rows, gate_input, norm_gain)
```

```python
import jax
import jax.numpy as jnp
from jax import lax
from jax.experimental import pallas as pl
from jax.experimental.pallas import tpu as pltpu
from jax.sharding import PartitionSpec as P

MESH = pl.DeviceIdType.MESH
F32 = jnp.float32
BF16 = jnp.bfloat16
HEADS = 32
T = 128
SLAB = 32
ZN = 8
BATCH = 4


def mm(a, b):
    return jnp.dot(a, b, preferred_element_type=F32)


def mmb(a, b):
    return mm(a.astype(BF16), b.astype(BF16))


def split(a):
    hi = a.astype(BF16)
    return hi, (a - hi.astype(F32)).astype(BF16)


def mm3(a, b):
    ah, al = split(a)
    bh, bl = split(b)
    first = mm(jnp.concatenate([ah, al], axis=1), jnp.concatenate([bh, bh], axis=0))
    return first + mm(ah, bl)


def mm_exact(a, b):
    bh, bl = split(b)
    return mm(jnp.concatenate([a, a], axis=1), jnp.concatenate([bh, bl], axis=0))


def bias_kernel(own_ref, out_ref, got, send_sem, recv_sem):
    ctx = lax.axis_index("context")
    hd = lax.axis_index("head")
    barrier = pltpu.get_barrier_semaphore()
    for s in range(1, 4):
        pl.semaphore_signal(
            barrier, inc=1, device_id=(ctx, lax.rem(hd + s, 4)), device_id_type=MESH
        )
    pl.semaphore_wait(barrier, 3)
    copies = []
    for s in range(1, 4):
        copy = pltpu.make_async_remote_copy(
            src_ref=own_ref,
            dst_ref=got.at[s - 1],
            send_sem=send_sem.at[s - 1],
            recv_sem=recv_sem.at[s - 1],
            device_id=(ctx, lax.rem(hd + s, 4)),
            device_id_type=MESH,
        )
        copy.start()
        copies.append(copy)
    for copy in copies:
        copy.wait()
    out_ref[...] = own_ref[...] + got[0] + got[1] + got[2]


def all_biases(decay_bias):
    hd = lax.axis_index("head")
    lanes = lax.broadcasted_iota(jnp.int32, (8, 128), 1)
    tiled = jnp.tile(decay_bias, 16)[None, :]
    own = jnp.where(lanes // 8 == hd, tiled, 0.0)
    vmem = pl.BlockSpec(memory_space=pltpu.VMEM)
    return pl.pallas_call(
        bias_kernel,
        out_shape=jax.ShapeDtypeStruct((8, 128), F32),
        in_specs=[vmem],
        out_specs=vmem,
        scratch_shapes=[
            pltpu.VMEM((3, 8, 128), F32),
            pltpu.SemaphoreType.DMA((3,)),
            pltpu.SemaphoreType.DMA((3,)),
        ],
        compiler_params=pltpu.CompilerParams(collective_id=0, has_side_effects=True),
    )(own)


def local_kernel(
    doc_ref, bias_ref, decay_ref, beta_ref, q_ref, k_ref, v_ref,
    ab_ref, r_ref, l_ref,
    pad, row_g, col_g, col_b, masks,
):
    step = pl.program_id(0)
    hd = lax.axis_index("head")
    keep0 = 1.0 - doc_ref[2 * hd].astype(F32)
    keep1 = 1.0 - doc_ref[2 * hd + 1].astype(F32)
    rows = lax.broadcasted_iota(jnp.int32, (T, T), 0)
    cols = lax.broadcasted_iota(jnp.int32, (T, T), 1)

    @pl.when(step == 0)
    def _():
        x = decay_ref[...] + bias_ref[0:1, 0:HEADS]
        tail = jnp.exp(-jnp.abs(x))
        one = 1.0 + tail
        away = one - 1.0
        exact = away == 0.0
        log1p = jnp.where(exact, tail, jnp.log(one) * (tail / jnp.where(exact, 1.0, away)))
        pad[...] = jnp.zeros((T, T), F32)
        pad[:, 0:HEADS] = -(jnp.maximum(x, 0.0) + log1p)
        lower = jnp.where(rows >= cols, 1.0, 0.0).astype(F32)
        cum = jnp.dot(
            lower, pad[...], preferred_element_type=F32, precision=lax.Precision.HIGHEST
        )
        row_g[...] = cum.T
        beta = 1.0 / (1.0 + jnp.exp(-beta_ref[...]))
        for h in range(HEADS):
            col_g[h] = jnp.broadcast_to(cum[:, h : h + 1], (T, T))
            col_b[h] = jnp.broadcast_to(beta[:, h : h + 1], (T, T))
        crossing = jnp.where((rows >= 64) & (cols < 64), keep1, 1.0)
        masks[0] = jnp.where(rows >= cols, crossing, 0.0)
        masks[1] = keep0 * jnp.where(rows >= 64, keep1, 1.0)
        masks[2] = jnp.where(cols >= 64, 1.0, keep1)

    inclusive = masks[0]
    reach = masks[1]
    leave = masks[2]

    def one_head(j):
        h = step * BATCH + j
        lanes = slice(j * 128, (j + 1) * 128)
        raw = k_ref[:, lanes].astype(F32)
        total = jnp.sum(raw * raw, axis=-1, keepdims=True)
        kf = (raw * lax.rsqrt(total + 1e-06)).astype(BF16).astype(F32)
        kt = kf.T
        kn = kf.astype(BF16)
        q = q_ref[:, lanes]
        cg = col_g[h]
        rg = row_g[pl.ds(h, 1), :]
        bt = col_b[h]
        decay = jnp.exp(jnp.minimum(cg - rg, 0.0)) * inclusive
        grams = mm(jnp.concatenate([kn, q], axis=0), kt.astype(BF16))
        low = jnp.where(rows > cols, bt * decay * grams[:T], 0.0)
        mix = decay * grams[T:]
        parts = []
        for b in range(16):
            block = low[8 * b : 8 * b + 8, :]
            x = jnp.where(rows[:8] + 8 * b == cols[:8], 1.0, 0.0).astype(F32)
            for c in range(7):
                x = x - block[:, 8 * b + c : 8 * b + c + 1] * x[c : c + 1, :]
            parts.append(x)
        x = jnp.concatenate(parts, axis=0)
        for small, large in ((8, 32), (32, 128)):
            off = (rows // small != cols // small) & (rows // large == cols // large)
            n = mmb(x, jnp.where(off, low, 0.0))
            nb = n.astype(BF16)
            y = x - mmb(nb, x)
            x = y + mmb(mm(nb, nb), y)
        e = jnp.exp(cg) * reach
        rhs = jnp.concatenate(
            [(bt * e * kf).astype(BF16), (bt * v_ref[:, lanes].astype(F32)).astype(BF16)], axis=1
        )
        wu = mmb(x, rhs).astype(BF16)
        last = cg[T - 1 : T, :]
        ends = kt * (jnp.exp(last - rg) * leave[0:1, :])
        both = mm(jnp.concatenate([mix.astype(BF16), ends.astype(BF16)], axis=0), wu)
        r_ref[j] = (e * q.astype(F32) - both[:T, :128]).astype(BF16)
        l_ref[j] = both[:T, 128:].astype(BF16)
        diag = jnp.where(rows == cols, 1.0 - jnp.exp(last) * (keep0 * keep1), 0.0)
        ab_ref[j, 0] = (diag + both[T:, :128]).astype(BF16)
        ab_ref[j, 1] = both[T:, 128:].astype(BF16)

    for j in range(BATCH):
        one_head(j)


def local_part(doc_start, biases, decay_logit, beta_logit, queries, key_input, value_input):
    wide = pl.BlockSpec((T, BATCH * 128), lambda g: (0, g))
    whole = lambda shape: pl.BlockSpec(shape, lambda g: (0,) * len(shape))
    head = pl.BlockSpec((BATCH, T, 128), lambda g: (g, 0, 0))
    return pl.pallas_call(
        local_kernel,
        grid=(HEADS // BATCH,),
        in_specs=[
            pl.BlockSpec(memory_space=pltpu.SMEM),
            whole((8, 128)), whole((T, HEADS)), whole((T, HEADS)),
            wide, wide, wide,
        ],
        out_specs=(pl.BlockSpec((BATCH, 2, 128, 128), lambda g: (g, 0, 0, 0)), head, head),
        out_shape=(
            jax.ShapeDtypeStruct((HEADS, 2, 128, 128), BF16),
            jax.ShapeDtypeStruct((HEADS, T, 128), BF16),
            jax.ShapeDtypeStruct((HEADS, T, 128), BF16),
        ),
        scratch_shapes=[
            pltpu.VMEM((T, T), F32),
            pltpu.VMEM((T, T), F32),
            pltpu.VMEM((HEADS, T, T), F32),
            pltpu.VMEM((HEADS, T, T), F32),
            pltpu.VMEM((3, T, T), F32),
        ],
        compiler_params=pltpu.CompilerParams(dimension_semantics=("arbitrary",)),
    )(doc_start, biases, decay_logit, beta_logit, queries, key_input, value_input)


def scan_kernel(
    ab_ref, out_ref,
    got, cur, pre_a, pre_b, blocks, zown, zgot, entry, stage,
    s1, r1, sz, rz, s3, r3,
):
    ctx = lax.axis_index("context")
    hd = lax.axis_index("head")
    z = ctx // 8
    xc = lax.rem(ctx, 8)
    me = xc * 4 + hd

    def peer(i):
        return (z * 8 + i // 4, lax.rem(i, 4))

    def zpeer(i):
        return (i * 8 + xc, hd)

    barrier = pltpu.get_barrier_semaphore()

    def greet(s, _):
        pl.semaphore_signal(
            barrier, inc=1, device_id=peer(lax.rem(me + s, SLAB)), device_id_type=MESH
        )
        return 0

    def zgreet(s, _):
        pl.semaphore_signal(
            barrier, inc=1, device_id=zpeer(lax.rem(z + s, ZN)), device_id_type=MESH
        )
        return 0

    lax.fori_loop(1, SLAB, greet, 0)
    lax.fori_loop(1, ZN, zgreet, 0)
    pl.semaphore_wait(barrier, SLAB - 1 + ZN - 1)

    def out_copy(i, slot):
        return pltpu.make_async_remote_copy(
            src_ref=ab_ref.at[i], dst_ref=got.at[slot],
            send_sem=s1.at[i], recv_sem=r1.at[slot],
            device_id=peer(i), device_id_type=MESH,
        )

    def z_copy(i, slot):
        return pltpu.make_async_remote_copy(
            src_ref=zown, dst_ref=zgot.at[slot],
            send_sem=sz.at[i], recv_sem=rz.at[slot],
            device_id=zpeer(i), device_id_type=MESH,
        )

    def back_copy(i, slot):
        return pltpu.make_async_remote_copy(
            src_ref=stage.at[i], dst_ref=out_ref.at[slot],
            send_sem=s3.at[i], recv_sem=r3.at[slot],
            device_id=peer(i), device_id_type=MESH,
        )

    def others(n, mine, act):
        def body(s, _):
            act(lax.rem(mine + s, n))
            return 0

        lax.fori_loop(1, n, body, 0)

    others(SLAB, me, lambda i: out_copy(i, me).start())
    got[me] = ab_ref[me]
    others(SLAB, me, lambda i: out_copy(i, i).wait_recv())

    eye = jnp.where(
        lax.broadcasted_iota(jnp.int32, (128, 128), 0)
        == lax.broadcasted_iota(jnp.int32, (128, 128), 1),
        1.0, 0.0,
    ).astype(BF16)
    for j in range(4):
        pre_a[8 * j] = jnp.concatenate([eye, jnp.zeros((128, 128), BF16)], axis=1)
        pre_b[8 * j] = jnp.zeros((128, 128), F32)
        cur[j, :, :128] = eye.astype(F32) - got[8 * j, 0].astype(F32)
        cur[j, :, 128:] = got[8 * j, 1].astype(F32)

    def extend(i, _):
        for j in range(4):
            now = cur[j]
            hi, lo = split(now)
            pre_a[8 * j + i] = jnp.concatenate([hi[:, :128], lo[:, :128]], axis=1)
            pre_b[8 * j + i] = now[:, 128:]
            a = got[8 * j + i, 0]
            b = got[8 * j + i, 1].astype(F32)
            new = now - mm(jnp.concatenate([a, a], axis=1), jnp.concatenate([hi, lo], axis=0))
            cur[j] = jnp.concatenate([new[:, :128], new[:, 128:] + b], axis=1)
        return 0

    lax.fori_loop(1, 8, extend, 0)

    def compose(later, earlier):
        new = mm3(later[:, :128], earlier)
        return jnp.concatenate([new[:, :128], new[:, 128:] + later[:, 128:]], axis=1)

    blocks[0] = cur[0]
    blocks[1] = compose(cur[1], blocks[0])
    blocks[2] = compose(cur[2], blocks[1])
    total = compose(cur[3], blocks[2])
    zown[0] = (eye.astype(F32) - total[:, :128]).astype(BF16)
    zown[1] = total[:, 128:].astype(BF16)
    others(ZN, z, lambda i: z_copy(i, z).start())
    entry[...] = jnp.zeros((128, 128), F32)
    others(ZN, z, lambda i: z_copy(i, i).wait_recv())

    def carry(i, _):
        before = entry[...]
        entry[...] = before - mm_exact(zgot[i, 0], before) + zgot[i, 1].astype(F32)
        return 0

    lax.fori_loop(0, z, carry, 0)

    first = entry[...]
    starts = [first]
    for j in range(3):
        starts.append(mm3(blocks[j][:, :128], first) + blocks[j][:, 128:])
    for j in range(4):
        hi = starts[j].astype(BF16)
        cur[j, :, :128] = hi.astype(F32)

    def spread(g):
        for c in range(4):
            i = lax.rem(me + 4 * g + c, SLAB)
            hi = cur[i // 8, :, :128].astype(BF16)
            value = mm(pre_a[i], jnp.concatenate([hi, hi], axis=0)) + pre_b[i]
            stage[i] = value.astype(BF16)

    def deliver(g, least):
        for c in range(least, 4):
            i = lax.rem(me + 4 * g + c, SLAB)
            back_copy(i, me).start()

    spread(0)
    spread(1)
    deliver(0, 1)

    def rest(g, _):
        spread(g)
        deliver(g - 1, 0)
        return 0

    lax.fori_loop(2, 8, rest, 0)
    out_ref[me] = stage[me]
    deliver(7, 0)
    others(SLAB, me, lambda i: back_copy(i, i).wait_recv())
    others(SLAB, me, lambda i: out_copy(i, me).wait_send())
    others(ZN, z, lambda i: z_copy(i, z).wait_send())
    others(SLAB, me, lambda i: back_copy(i, me).wait_send())


def entering_states(ab):
    vmem = pl.BlockSpec(memory_space=pltpu.VMEM)
    dma = pltpu.SemaphoreType.DMA
    return pl.pallas_call(
        scan_kernel,
        out_shape=jax.ShapeDtypeStruct((HEADS, 128, 128), BF16),
        in_specs=[vmem],
        out_specs=vmem,
        scratch_shapes=[
            pltpu.VMEM((SLAB, 2, 128, 128), BF16),
            pltpu.VMEM((4, 128, 256), F32),
            pltpu.VMEM((SLAB, 128, 256), BF16),
            pltpu.VMEM((SLAB, 128, 128), F32),
            pltpu.VMEM((3, 128, 256), F32),
            pltpu.VMEM((2, 128, 128), BF16),
            pltpu.VMEM((ZN, 2, 128, 128), BF16),
            pltpu.VMEM((128, 128), F32),
            pltpu.VMEM((SLAB, 128, 128), BF16),
            dma((SLAB,)), dma((SLAB,)), dma((ZN,)), dma((ZN,)), dma((SLAB,)), dma((SLAB,)),
        ],
        compiler_params=pltpu.CompilerParams(collective_id=1, has_side_effects=True),
    )(ab)


def out_kernel(gain_ref, r_ref, l_ref, s_ref, gate_ref, o_ref):
    gain = gain_ref[0:1, :]
    for j in range(BATCH):
        lanes = slice(j * 128, (j + 1) * 128)
        core = (l_ref[j].astype(F32) + mm(r_ref[j], s_ref[j])).astype(BF16).astype(F32)
        mean = jnp.sum(core * core, axis=-1, keepdims=True) * (1.0 / 128)
        gate = gate_ref[:, lanes].astype(F32)
        silu = gate / (1.0 + jnp.exp(-gate))
        o_ref[:, lanes] = (core * lax.rsqrt(mean + 1e-06) * gain * silu).astype(BF16)


def outputs(norm_gain, r, lo, states, gate_input):
    wide = pl.BlockSpec((T, BATCH * 128), lambda g: (0, g))
    head = pl.BlockSpec((BATCH, T, 128), lambda g: (g, 0, 0))
    return pl.pallas_call(
        out_kernel,
        grid=(HEADS // BATCH,),
        in_specs=[pl.BlockSpec((1, 128), lambda g: (0, 0)), head, head, head, wide],
        out_specs=wide,
        out_shape=jax.ShapeDtypeStruct(gate_input.shape, BF16),
        compiler_params=pltpu.CompilerParams(dimension_semantics=("arbitrary",)),
    )(norm_gain[None, :], r, lo, states, gate_input)


def body(
    queries, key_input, value_input, gate_input,
    decay_logit, beta_logit, decay_bias, norm_gain, doc_start,
):
    biases = all_biases(decay_bias)
    ab, r, lo = local_part(
        doc_start, biases, decay_logit, beta_logit, queries, key_input, value_input
    )
    states = entering_states(ab)
    return outputs(norm_gain, r, lo, states, gate_input)


def solution(mesh):
    rows = P(("context", "head"), None)
    return jax.shard_map(
        body,
        mesh=mesh,
        in_specs=(rows, rows, rows, rows, rows, rows, P("head"), P(), P("context")),
        out_specs=rows,
        check_vma=False,
    )
```

```python
import jax
import jax.numpy as jnp
from jax import lax
from jax.experimental import pallas as pl
from jax.experimental.pallas import tpu as pltpu
from jax.sharding import PartitionSpec as P

MESH = pl.DeviceIdType.MESH
F32 = jnp.float32
BF16 = jnp.bfloat16
HEADS = 32
T = 128
SLAB = 32
ZN = 8
BATCH = 4
EARLY = 3


def mm(a, b):
    return jnp.dot(a, b, preferred_element_type=F32)


def mmb(a, b):
    return mm(a.astype(BF16), b.astype(BF16))


def split(a):
    hi = a.astype(BF16)
    return hi, (a - hi.astype(F32)).astype(BF16)


def mm3(a, b):
    ah, al = split(a)
    bh, bl = split(b)
    first = mm(jnp.concatenate([ah, al], axis=1), jnp.concatenate([bh, bh], axis=0))
    return first + mm(ah, bl)


def mm_exact(a, b):
    bh, bl = split(b)
    return mm(jnp.concatenate([a, a], axis=1), jnp.concatenate([bh, bl], axis=0))


def off_block(rows, cols, small, large):
    return (rows // small != cols // small) & (rows // large == cols // large)


def inverse8(low, rows, cols):
    block = jnp.where(rows // 8 == cols // 8, low, 0.0)
    x = jnp.where(rows == cols, 1.0, 0.0).astype(F32).reshape(16, 8, T)
    for c in range(7):
        factor = jnp.sum(jnp.where(cols % 8 == c, block, 0.0), axis=1, keepdims=True)
        x = x - factor.reshape(16, 8, 1) * x[:, c : c + 1, :]
    return x.reshape(T, T)


def diagonal(m):
    zero = jnp.zeros((T, T), BF16)
    top = jnp.concatenate([m[:, :T], zero], axis=1)
    return jnp.concatenate([top, jnp.concatenate([zero, m[:, T:]], axis=1)], axis=0)


def invert_pair(low_a, low_b, rows, cols):
    x = jnp.concatenate([inverse8(low_a, rows, cols), inverse8(low_b, rows, cols)], axis=1)
    for small, large in ((8, 32), (32, 128)):
        off = off_block(rows, cols, small, large)
        low = jnp.concatenate(
            [jnp.where(off, low_a, 0.0).astype(BF16), jnp.where(off, low_b, 0.0).astype(BF16)],
            axis=1,
        )
        xb = x.astype(BF16)
        n = mm(xb, diagonal(low)).astype(BF16)
        y = x - mm(n, diagonal(xb))
        x = y + mm(mm(n, diagonal(n)).astype(BF16), diagonal(y.astype(BF16)))
    return x[:, :T], x[:, T:]


def layer_kernel(
    doc_ref, own_bias, decay_ref, beta_ref, gain_ref, q_hbm, k_hbm, v_hbm, gate_hbm,
    o_ref,
    q_ref, k_ref, v_ref, gate_ref, bias, pad, row_g, col_g, col_b, masks,
    kts, wus, rs, ls,
    ab_ref, got, cur, pre_a, pre_b, blocks, zown, zgot, entry, stage, arrived,
    sin, sb, rb, s1, r1, sz, rz, s3, r3,
):
    ctx = lax.axis_index("context")
    hd = lax.axis_index("head")
    z = ctx // 8
    xc = lax.rem(ctx, 8)
    me = xc * 4 + hd

    loads = [
        pltpu.make_async_copy(a, b, sin.at[n])
        for n, (a, b) in enumerate(
            ((k_hbm, k_ref), (v_hbm, v_ref), (q_hbm, q_ref), (gate_hbm, gate_ref))
        )
    ]
    for load in loads:
        load.start()

    def peer(i):
        return (z * 8 + i // 4, lax.rem(i, 4))

    def zpeer(i):
        return (i * 8 + xc, hd)

    def others(n, mine, act):
        def step(s, _):
            act(lax.rem(mine + s, n))
            return 0

        lax.fori_loop(1, n, step, 0)

    barrier = pltpu.get_barrier_semaphore()

    def greet(device):
        pl.semaphore_signal(barrier, inc=1, device_id=device, device_id_type=MESH)

    others(SLAB, me, lambda i: greet(peer(i)))
    others(ZN, z, lambda i: greet(zpeer(i)))
    pl.semaphore_wait(barrier, SLAB - 1 + ZN - 1)

    def remote(src, dst, send, recv, device):
        return pltpu.make_async_remote_copy(
            src_ref=src, dst_ref=dst, send_sem=send, recv_sem=recv,
            device_id=device, device_id_type=MESH,
        )

    def bias_copy(i, slot):
        return remote(own_bias, bias.at[slot], sb.at[i], rb.at[slot], (ctx, i))

    def out_copy(i, slot):
        return remote(ab_ref.at[i], got.at[slot], s1.at[i], r1.at[slot], peer(i))

    def z_copy(i, slot):
        return remote(zown, zgot.at[slot], sz.at[i], rz.at[slot], zpeer(i))

    def back_copy(i, slot):
        return remote(stage.at[i], arrived.at[slot], s3.at[i], r3.at[slot], peer(i))

    others(4, hd, lambda i: bias_copy(i, hd).start())
    bias[hd] = own_bias[...]

    rows = lax.broadcasted_iota(jnp.int32, (T, T), 0)
    cols = lax.broadcasted_iota(jnp.int32, (T, T), 1)
    keep0 = 1.0 - doc_ref[2 * hd].astype(F32)
    keep1 = 1.0 - doc_ref[2 * hd + 1].astype(F32)
    masks[0] = jnp.where(rows >= cols, jnp.where((rows >= 64) & (cols < 64), keep1, 1.0), 0.0)
    masks[1] = keep0 * jnp.where(rows >= 64, keep1, 1.0)
    masks[2] = jnp.where(cols >= 64, 1.0, keep1)
    pad[HEADS : 2 * HEADS] = 1.0 / (1.0 + jnp.exp(-beta_ref[...]))
    pad[2 * HEADS :] = jnp.zeros((2 * HEADS, T), F32)

    others(4, hd, lambda i: bias_copy(i, i).wait_recv())
    x = decay_ref[...] + bias[...].reshape(HEADS, T)
    tail = jnp.exp(-jnp.abs(x))
    one = 1.0 + tail
    away = one - 1.0
    exact = away == 0.0
    log1p = jnp.where(exact, tail, jnp.log(one) * (tail / jnp.where(exact, 1.0, away)))
    upper = jnp.where(rows <= cols, 1.0, 0.0).astype(F32)
    cum = jnp.dot(
        -(jnp.maximum(x, 0.0) + log1p), upper,
        preferred_element_type=F32, precision=lax.Precision.HIGHEST,
    )
    row_g[...] = cum
    pad[0:HEADS] = cum
    by_token = pad[...].T
    for h in range(HEADS):
        col_g[h] = jnp.broadcast_to(by_token[:, h : h + 1], (T, T))
        col_b[h] = jnp.broadcast_to(by_token[:, HEADS + h : HEADS + h + 1], (T, T))

    loads[0].wait()
    loads[1].wait()

    def lanes_of(h):
        return pl.ds(pl.multiple_of(h * 128, 128), 128)

    def decay_of(h):
        gap = col_g[h] - row_g[pl.ds(h, 1), :]
        return jnp.exp(jnp.minimum(gap, 0.0)) * masks[0]

    def maps(g, _):
        @pl.when(g > 0)
        def _():
            for c in range(BATCH):
                i = lax.rem(me + 1 + BATCH * (g - 1) + c, SLAB)
                out_copy(i, me).start()

        heads = [lax.rem(me + 1 + BATCH * g + c, SLAB) for c in range(BATCH)]
        lows, keys, turned = [], [], []
        for h in heads:
            raw = k_ref[:, lanes_of(h)].astype(F32)
            total = jnp.sum(raw * raw, axis=-1, keepdims=True)
            kn = (raw * lax.rsqrt(total + 1e-06)).astype(BF16)
            kf = kn.astype(F32)
            kt = kf.T
            kb = kt.astype(BF16)
            kts[h] = kb
            low = jnp.where(rows > cols, col_b[h] * decay_of(h) * mm(kn, kb), 0.0)
            lows.append(low)
            keys.append(kf)
            turned.append(kt)
        inverses = []
        for c in range(0, BATCH, 2):
            inverses += list(invert_pair(lows[c], lows[c + 1], rows, cols))
        for c, h in enumerate(heads):
            bt = col_b[h]
            e = jnp.exp(col_g[h]) * masks[1]
            rhs = jnp.concatenate(
                [
                    (bt * e * keys[c]).astype(BF16),
                    (bt * v_ref[:, lanes_of(h)].astype(F32)).astype(BF16),
                ],
                axis=1,
            )
            wu = mmb(inverses[c], rhs).astype(BF16)
            wus[h] = wu
            rg = row_g[pl.ds(h, 1), :]
            last = col_g[h, T - 1 : T, :]
            ends = turned[c] * (jnp.exp(last - rg) * masks[2, 0:1, :])
            both = mm(ends.astype(BF16), wu)
            diag = jnp.where(rows == cols, 1.0 - jnp.exp(last) * (keep0 * keep1), 0.0)
            ab_ref[h, 0] = (diag + both[:, :128]).astype(BF16)
            ab_ref[h, 1] = both[:, 128:].astype(BF16)
        return 0

    steps = HEADS // BATCH
    lax.fori_loop(0, steps, maps, 0)
    for c in range(BATCH - 1):
        out_copy(lax.rem(me + 1 + BATCH * (steps - 1) + c, SLAB), me).start()
    got[me] = ab_ref[me]

    def reads(g, _):
        for c in range(4):
            h = 4 * g + c
            q = q_ref[:, lanes_of(h)]
            mix = decay_of(h) * mm(q, kts[h])
            both = mmb(mix, wus[h])
            e = jnp.exp(col_g[h]) * masks[1]
            rs[h] = (e * q.astype(F32) - both[:, :128]).astype(BF16)
            ls[h] = both[:, 128:]
        return 0

    loads[2].wait()
    lax.fori_loop(0, EARLY, reads, 0)
    others(SLAB, me, lambda i: out_copy(i, i).wait_recv())

    eye = jnp.where(rows == cols, 1.0, 0.0).astype(F32)
    for j in range(4):
        pre_a[8 * j, :, :128] = eye.astype(BF16)
        pre_a[8 * j, :, 128:] = jnp.zeros((128, 128), BF16)
        pre_b[8 * j] = jnp.zeros((128, 128), F32)
        cur[j, :, :128] = eye - got[8 * j, 0].astype(F32)
        cur[j, :, 128:] = got[8 * j, 1].astype(F32)

    def extend(i, _):
        for j in range(4):
            now = cur[j]
            hi, lo = split(now)
            pre_a[8 * j + i] = jnp.concatenate([hi[:, :128], lo[:, :128]], axis=1)
            pre_b[8 * j + i] = now[:, 128:]
            a = got[8 * j + i, 0]
            b = got[8 * j + i, 1].astype(F32)
            new = now - mm(jnp.concatenate([a, a], axis=1), jnp.concatenate([hi, lo], axis=0))
            cur[j] = jnp.concatenate([new[:, :128], new[:, 128:] + b], axis=1)
        return 0

    lax.fori_loop(1, 8, extend, 0)

    def compose(later, earlier):
        new = mm3(later[:, :128], earlier)
        return jnp.concatenate([new[:, :128], new[:, 128:] + later[:, 128:]], axis=1)

    blocks[0] = cur[0]
    blocks[1] = compose(cur[1], blocks[0])
    blocks[2] = compose(cur[2], blocks[1])
    total = compose(cur[3], blocks[2])
    zown[0] = (eye - total[:, :128]).astype(BF16)
    zown[1] = total[:, 128:].astype(BF16)
    others(ZN, z, lambda i: z_copy(i, z).start())
    entry[...] = jnp.zeros((128, 128), F32)
    lax.fori_loop(EARLY, 8, reads, 0)
    others(ZN, z, lambda i: z_copy(i, i).wait_recv())

    def carry(i, _):
        before = entry[...]
        entry[...] = before - mm_exact(zgot[i, 0], before) + zgot[i, 1].astype(F32)
        return 0

    lax.fori_loop(0, z, carry, 0)

    first = entry[...]
    starts = [first]
    for j in range(3):
        starts.append(mm3(blocks[j][:, :128], first) + blocks[j][:, 128:])
    for j in range(4):
        cur[j, :, :128] = starts[j].astype(BF16).astype(F32)

    def spread(g):
        for c in range(4):
            i = lax.rem(me + 4 * g + c, SLAB)
            hi = cur[i // 8, :, :128].astype(BF16)
            value = mm(pre_a[i], jnp.concatenate([hi, hi], axis=0)) + pre_b[i]
            stage[i] = value.astype(BF16)

    def deliver(g, least):
        for c in range(least, 4):
            back_copy(lax.rem(me + 4 * g + c, SLAB), me).start()

    spread(0)
    spread(1)
    deliver(0, 1)

    def rest(g, _):
        spread(g)
        deliver(g - 1, 0)
        return 0

    lax.fori_loop(2, 8, rest, 0)
    arrived[me] = stage[me]
    deliver(7, 0)
    loads[3].wait()

    def finish(g, least):
        heads = [lax.rem(me + SLAB - (4 * g + c), SLAB) for c in range(4)]
        for i in heads[least:]:
            back_copy(i, i).wait_recv()
        for h in heads:
            core = (ls[h] + mm(rs[h], arrived[h])).astype(BF16).astype(F32)
            mean = jnp.sum(core * core, axis=-1, keepdims=True) * (1.0 / 128)
            gate = gate_ref[:, lanes_of(h)].astype(F32)
            silu = gate / (1.0 + jnp.exp(-gate))
            scaled = core * lax.rsqrt(mean + 1e-06) * gain_ref[...]
            o_ref[:, lanes_of(h)] = (scaled * silu).astype(BF16)

    finish(0, 1)

    def finish_rest(g, _):
        finish(g, 0)
        return 0

    lax.fori_loop(1, 8, finish_rest, 0)
    others(4, hd, lambda i: bias_copy(i, hd).wait_send())
    others(SLAB, me, lambda i: out_copy(i, me).wait_send())
    others(ZN, z, lambda i: z_copy(i, z).wait_send())
    others(SLAB, me, lambda i: back_copy(i, me).wait_send())


def body(
    queries, key_input, value_input, gate_input,
    decay_logit, beta_logit, decay_bias, norm_gain, doc_start,
):
    vmem = pl.BlockSpec(memory_space=pltpu.VMEM)
    hbm = pl.BlockSpec(memory_space=pl.ANY)
    dma = pltpu.SemaphoreType.DMA
    rows = pltpu.VMEM((T, HEADS * 128), BF16)
    square = pltpu.VMEM((T, T), F32)
    return pl.pallas_call(
        layer_kernel,
        out_shape=jax.ShapeDtypeStruct(gate_input.shape, BF16),
        in_specs=[pl.BlockSpec(memory_space=pltpu.SMEM)] + [vmem] * 4 + [hbm] * 4,
        out_specs=vmem,
        scratch_shapes=[
            rows, rows, rows, rows,
            pltpu.VMEM((4, 8, T), F32),
            square,
            pltpu.VMEM((HEADS, T), F32),
            pltpu.VMEM((HEADS, T, T), F32),
            pltpu.VMEM((HEADS, T, T), F32),
            pltpu.VMEM((3, T, T), F32),
            pltpu.VMEM((HEADS, 128, T), BF16),
            pltpu.VMEM((HEADS, T, 256), BF16),
            pltpu.VMEM((HEADS, T, 128), BF16),
            pltpu.VMEM((HEADS, T, 128), F32),
            pltpu.VMEM((HEADS, 2, 128, 128), BF16),
            pltpu.VMEM((SLAB, 2, 128, 128), BF16),
            pltpu.VMEM((4, 128, 256), F32),
            pltpu.VMEM((SLAB, 128, 256), BF16),
            pltpu.VMEM((SLAB, 128, 128), F32),
            pltpu.VMEM((3, 128, 256), F32),
            pltpu.VMEM((2, 128, 128), BF16),
            pltpu.VMEM((ZN, 2, 128, 128), BF16),
            pltpu.VMEM((128, 128), F32),
            pltpu.VMEM((SLAB, 128, 128), BF16),
            pltpu.VMEM((SLAB, 128, 128), BF16),
            dma((4,)), dma((4,)), dma((4,)),
            dma((SLAB,)), dma((SLAB,)), dma((ZN,)), dma((ZN,)), dma((SLAB,)), dma((SLAB,)),
        ],
        compiler_params=pltpu.CompilerParams(collective_id=0, has_side_effects=True),
    )(
        doc_start,
        jnp.broadcast_to(decay_bias[:, None], (8, T)),
        decay_logit.T, beta_logit.T, norm_gain[None, :],
        queries, key_input, value_input, gate_input,
    )


def solution(mesh):
    rows = P(("context", "head"), None)
    return jax.shard_map(
        body,
        mesh=mesh,
        in_specs=(rows, rows, rows, rows, rows, rows, P("head"), P(), P("context")),
        out_specs=rows,
        check_vma=False,
    )
```

```python
import jax
import jax.numpy as jnp
from jax import lax
from jax.experimental import pallas as pl
from jax.experimental.pallas import tpu as pltpu
from jax.sharding import PartitionSpec as P

MESH = pl.DeviceIdType.MESH
F32 = jnp.float32
BF16 = jnp.bfloat16
HEADS = 32
T = 128
SLAB = 32
ZN = 8
BATCH = 4
EARLY = 2
STRIDE = 11


def mm(a, b):
    return jnp.dot(a, b, preferred_element_type=F32)


def mmb(a, b):
    return mm(a.astype(BF16), b.astype(BF16))


def split(a):
    hi = a.astype(BF16)
    return hi, (a - hi.astype(F32)).astype(BF16)


def mm3(a, b):
    ah, al = split(a)
    bh, bl = split(b)
    first = mm(jnp.concatenate([ah, al], axis=1), jnp.concatenate([bh, bh], axis=0))
    return first + mm(ah, bl)


def mm_exact(a, b):
    bh, bl = split(b)
    return mm(jnp.concatenate([a, a], axis=1), jnp.concatenate([bh, bl], axis=0))


def off_block(rows, cols, small, large):
    return (rows // small != cols // small) & (rows // large == cols // large)


def inverse8(low, rows, cols):
    block = jnp.where(rows // 8 == cols // 8, low, 0.0)
    x = jnp.where(rows == cols, 1.0, 0.0).astype(F32).reshape(16, 8, T)
    for c in range(7):
        factor = jnp.sum(jnp.where(cols % 8 == c, block, 0.0), axis=1, keepdims=True)
        x = x - factor.reshape(16, 8, 1) * x[:, c : c + 1, :]
    return x.reshape(T, T)


def diagonal(m):
    zero = jnp.zeros((T, T), BF16)
    top = jnp.concatenate([m[:, :T], zero], axis=1)
    return jnp.concatenate([top, jnp.concatenate([zero, m[:, T:]], axis=1)], axis=0)


def invert_pair(low_a, low_b, rows, cols):
    x = jnp.concatenate([inverse8(low_a, rows, cols), inverse8(low_b, rows, cols)], axis=1)
    for small, large in ((8, 32), (32, 128)):
        off = off_block(rows, cols, small, large)
        low = jnp.concatenate(
            [jnp.where(off, low_a, 0.0).astype(BF16), jnp.where(off, low_b, 0.0).astype(BF16)],
            axis=1,
        )
        xb = x.astype(BF16)
        n = mm(xb, diagonal(low)).astype(BF16)
        y = x - mm(n, diagonal(xb))
        x = y + mm(mm(n, diagonal(n)).astype(BF16), diagonal(y.astype(BF16)))
    return x[:, :T], x[:, T:]


def layer_kernel(
    doc_ref, bias_ref, decay_ref, beta_ref, gain_ref, q_hbm, k_hbm, v_hbm, gate_hbm,
    o_ref,
    q_ref, k_ref, v_ref, gate_ref, own_bias, bias, gates, pad, tokens, row_g, col_g, col_b, masks,
    kns, kts, wus, rs, ls,
    ab_ref, got, cur, pre_a, pre_b, blocks, zown, zgot, entry, stage, arrived,
    sin, sb, rb, s1, r1, sz, rz, s3, r3,
):
    ctx = lax.axis_index("context")
    hd = lax.axis_index("head")
    z = ctx // 8
    xc = lax.rem(ctx, 8)
    me = xc * 4 + hd

    loads = [
        pltpu.make_async_copy(a, b, sin.at[n])
        for n, (a, b) in enumerate(
            ((k_hbm, k_ref), (v_hbm, v_ref), (q_hbm, q_ref), (gate_hbm, gate_ref))
        )
    ]
    for load in loads:
        load.start()

    def peer(i):
        return (z * 8 + i // 4, lax.rem(i, 4))

    def turn(k):
        return lax.rem(me + STRIDE * k, SLAB)

    def zpeer(i):
        return (i * 8 + xc, hd)

    def others(n, mine, act):
        def step(s, _):
            act(lax.rem(mine + s, n))
            return 0

        lax.fori_loop(1, n, step, 0)

    def later(act):
        def step(i, _):
            act(i)
            return 0

        lax.fori_loop(z + 1, ZN, step, 0)

    barrier = pltpu.get_barrier_semaphore()

    def greet(device):
        pl.semaphore_signal(barrier, inc=1, device_id=device, device_id_type=MESH)

    others(SLAB, me, lambda i: greet(peer(i)))
    others(ZN, z, lambda i: greet(zpeer(i)))

    def remote(src, dst, send, recv, device):
        return pltpu.make_async_remote_copy(
            src_ref=src, dst_ref=dst, send_sem=send, recv_sem=recv,
            device_id=device, device_id_type=MESH,
        )

    def bias_copy(i, slot):
        return remote(own_bias, bias.at[slot], sb.at[i], rb.at[slot], (ctx, i))

    def out_copy(i, slot):
        return remote(ab_ref.at[i], got.at[slot], s1.at[i], r1.at[slot], peer(i))

    def z_copy(i, slot):
        return remote(zown, zgot.at[slot], sz.at[i], rz.at[slot], zpeer(i))

    def back_copy(i, slot):
        return remote(stage.at[i], arrived.at[slot], s3.at[i], r3.at[slot], peer(i))

    rows = lax.broadcasted_iota(jnp.int32, (T, T), 0)
    cols = lax.broadcasted_iota(jnp.int32, (T, T), 1)
    keep0 = 1.0 - doc_ref[2 * hd].astype(F32)
    keep1 = 1.0 - doc_ref[2 * hd + 1].astype(F32)
    for r in range(8):
        own_bias[r : r + 1, :] = jnp.full((1, T), bias_ref[r], F32)
    masks[0] = jnp.where(rows >= cols, jnp.where((rows >= 64) & (cols < 64), keep1, 1.0), 0.0)
    masks[1] = keep0 * jnp.where(rows >= 64, keep1, 1.0)
    masks[2] = jnp.where(cols >= 64, 1.0, keep1)
    gates[...] = 1.0 / (1.0 + jnp.exp(-beta_ref[...]))
    pad[2 * HEADS :] = jnp.zeros((2 * HEADS, T), F32)

    pl.semaphore_wait(barrier, SLAB - 1 + ZN - 1)
    others(4, hd, lambda i: bias_copy(i, hd).start())
    bias[hd] = own_bias[...]

    def lanes_of(h):
        return pl.ds(pl.multiple_of(h * 128, 128), 128)

    loads[0].wait()

    def normalize(g):
        for c in range(BATCH):
            h = turn(1 + BATCH * g + c)
            raw = k_ref[:, lanes_of(h)].astype(F32)
            total = jnp.sum(raw * raw, axis=-1, keepdims=True)
            kn = (raw * lax.rsqrt(total + 1e-06)).astype(BF16)
            kns[h] = kn
            kts[h] = kn.astype(F32).T.astype(BF16)

    normalize(0)
    others(4, hd, lambda i: bias_copy(i, i).wait_recv())
    x = decay_ref[...] + bias[...].reshape(HEADS, T)
    tail = jnp.exp(-jnp.abs(x))
    one = 1.0 + tail
    away = one - 1.0
    exact = away == 0.0
    log1p = jnp.where(exact, tail, jnp.log(one) * (tail / jnp.where(exact, 1.0, away)))
    upper = jnp.where(rows <= cols, 1.0, 0.0).astype(F32)
    cum = jnp.dot(
        -(jnp.maximum(x, 0.0) + log1p), upper,
        preferred_element_type=F32, precision=lax.Precision.HIGHEST,
    )
    row_g[...] = cum
    for k in range(HEADS):
        row = pl.ds(turn(k + 1), 1)
        pad[k : k + 1] = row_g[row, :]
        pad[HEADS + k : HEADS + k + 1] = gates[row, :]
    tokens[...] = pad[...].T

    loads[1].wait()

    def decay_of(h):
        gap = col_g[h] - row_g[pl.ds(h, 1), :]
        return jnp.exp(jnp.minimum(gap, 0.0)) * masks[0]

    def maps(g, _):
        @pl.when(g > 0)
        def _():
            for c in range(BATCH):
                i = turn(1 + BATCH * (g - 1) + c)
                out_copy(i, me).start()

        heads = [turn(1 + BATCH * g + c) for c in range(BATCH)]
        normalize(g + 1)
        lanes = tokens[...]
        for c, h in enumerate(heads):
            col_g[h] = jnp.broadcast_to(lanes[:, c : c + 1], (T, T))
            col_b[h] = jnp.broadcast_to(lanes[:, HEADS + c : HEADS + c + 1], (T, T))
        tokens[...] = jnp.concatenate([lanes[:, BATCH:], lanes[:, :BATCH]], axis=1)
        lows = []
        for h in heads:
            gram = mm(kns[h], kts[h])
            lows.append(jnp.where(rows > cols, col_b[h] * decay_of(h) * gram, 0.0))
        inverses = []
        for c in range(0, BATCH, 2):
            inverses += list(invert_pair(lows[c], lows[c + 1], rows, cols))
        for c, h in enumerate(heads):
            bt = col_b[h]
            e = jnp.exp(col_g[h]) * masks[1]
            rhs = jnp.concatenate(
                [
                    (bt * e * kns[h].astype(F32)).astype(BF16),
                    (bt * v_ref[:, lanes_of(h)].astype(F32)).astype(BF16),
                ],
                axis=1,
            )
            wu = mmb(inverses[c], rhs).astype(BF16)
            wus[h] = wu
            rg = row_g[pl.ds(h, 1), :]
            last = col_g[h, T - 1 : T, :]
            ends = kts[h].astype(F32) * (jnp.exp(last - rg) * masks[2, 0:1, :])
            both = mm(ends.astype(BF16), wu)
            diag = jnp.where(rows == cols, 1.0 - jnp.exp(last) * (keep0 * keep1), 0.0)
            ab_ref[h, 0] = (diag + both[:, :128]).astype(BF16)
            ab_ref[h, 1] = both[:, 128:].astype(BF16)
        return 0

    steps = HEADS // BATCH
    lax.fori_loop(0, steps, maps, 0)
    for c in range(BATCH - 1):
        out_copy(turn(1 + BATCH * (steps - 1) + c), me).start()
    got[me] = ab_ref[me]

    def reads(g, _):
        for c in range(4):
            h = 4 * g + c
            q = q_ref[:, lanes_of(h)]
            mix = decay_of(h) * mm(q, kts[h])
            both = mmb(mix, wus[h])
            e = jnp.exp(col_g[h]) * masks[1]
            rs[h] = (e * q.astype(F32) - both[:, :128]).astype(BF16)
            ls[h] = both[:, 128:]
        return 0

    loads[2].wait()
    lax.fori_loop(0, EARLY, reads, 0)
    others(SLAB, me, lambda i: out_copy(i, i).wait_recv())

    eye = jnp.where(rows == cols, 1.0, 0.0).astype(F32)
    for j in range(4):
        pre_a[8 * j, :, :128] = eye.astype(BF16)
        pre_a[8 * j, :, 128:] = jnp.zeros((128, 128), BF16)
        pre_b[8 * j] = jnp.zeros((128, 128), F32)
        cur[j, :, :128] = eye - got[8 * j, 0].astype(F32)
        cur[j, :, 128:] = got[8 * j, 1].astype(F32)

    def extend(i, _):
        for j in range(4):
            now = cur[j]
            hi, lo = split(now)
            pre_a[8 * j + i] = jnp.concatenate([hi[:, :128], lo[:, :128]], axis=1)
            pre_b[8 * j + i] = now[:, 128:]
            a = got[8 * j + i, 0]
            b = got[8 * j + i, 1].astype(F32)
            new = now - mm(jnp.concatenate([a, a], axis=1), jnp.concatenate([hi, lo], axis=0))
            cur[j] = jnp.concatenate([new[:, :128], new[:, 128:] + b], axis=1)
        return 0

    lax.fori_loop(1, 8, extend, 0)

    def compose(later, earlier):
        new = mm3(later[:, :128], earlier)
        return jnp.concatenate([new[:, :128], new[:, 128:] + later[:, 128:]], axis=1)

    blocks[0] = cur[0]
    blocks[1] = compose(cur[1], blocks[0])
    blocks[2] = compose(cur[2], blocks[1])
    total = compose(cur[3], blocks[2])
    zown[0] = (eye - total[:, :128]).astype(BF16)
    zown[1] = total[:, 128:].astype(BF16)
    later(lambda i: z_copy(i, z).start())
    entry[...] = jnp.zeros((128, 128), F32)
    lax.fori_loop(EARLY, 8, reads, 0)

    def carry(i, _):
        z_copy(i, i).wait_recv()
        before = entry[...]
        entry[...] = before - mm_exact(zgot[i, 0], before) + zgot[i, 1].astype(F32)
        return 0

    lax.fori_loop(0, z, carry, 0)

    first = entry[...]
    starts = [first]
    for j in range(3):
        starts.append(mm3(blocks[j][:, :128], first) + blocks[j][:, 128:])
    for j in range(4):
        cur[j, :, :128] = starts[j].astype(BF16).astype(F32)

    def spread(g):
        for c in range(4):
            i = turn(4 * g + c)
            hi = cur[i // 8, :, :128].astype(BF16)
            value = mm(pre_a[i], jnp.concatenate([hi, hi], axis=0)) + pre_b[i]
            stage[i] = value.astype(BF16)

    def deliver(g, least):
        for c in range(least, 4):
            back_copy(turn(4 * g + c), me).start()

    spread(0)
    spread(1)
    deliver(0, 1)

    def rest(g, _):
        spread(g)
        deliver(g - 1, 0)
        return 0

    lax.fori_loop(2, 8, rest, 0)
    arrived[me] = stage[me]
    deliver(7, 0)
    loads[3].wait()

    def finish(g, least):
        heads = [turn(SLAB - (4 * g + c)) for c in range(4)]
        for i in heads[least:]:
            back_copy(i, i).wait_recv()
        for h in heads:
            core = (ls[h] + mm(rs[h], arrived[h])).astype(BF16).astype(F32)
            mean = jnp.sum(core * core, axis=-1, keepdims=True) * (1.0 / 128)
            gate = gate_ref[:, lanes_of(h)].astype(F32)
            silu = gate / (1.0 + jnp.exp(-gate))
            scaled = core * lax.rsqrt(mean + 1e-06) * gain_ref[...]
            o_ref[:, lanes_of(h)] = (scaled * silu).astype(BF16)

    finish(0, 1)

    def finish_rest(g, _):
        finish(g, 0)
        return 0

    lax.fori_loop(1, 8, finish_rest, 0)
    others(4, hd, lambda i: bias_copy(i, hd).wait_send())
    others(SLAB, me, lambda i: out_copy(i, me).wait_send())
    later(lambda i: z_copy(i, z).wait_send())
    others(SLAB, me, lambda i: back_copy(i, me).wait_send())


def body(
    queries, key_input, value_input, gate_input,
    decay_logit, beta_logit, decay_bias, norm_gain, doc_start,
):
    smem = pl.BlockSpec(memory_space=pltpu.SMEM)
    vmem = pl.BlockSpec(memory_space=pltpu.VMEM)
    hbm = pl.BlockSpec(memory_space=pl.ANY)
    dma = pltpu.SemaphoreType.DMA
    rows = pltpu.VMEM((T, HEADS * 128), BF16)
    square = pltpu.VMEM((T, T), F32)
    return pl.pallas_call(
        layer_kernel,
        out_shape=jax.ShapeDtypeStruct(gate_input.shape, BF16),
        in_specs=[smem] * 2 + [vmem] * 3 + [hbm] * 4,
        out_specs=vmem,
        scratch_shapes=[
            rows, rows, rows, rows,
            pltpu.VMEM((8, T), F32),
            pltpu.VMEM((4, 8, T), F32),
            pltpu.VMEM((HEADS, T), F32),
            square,
            square,
            pltpu.VMEM((HEADS, T), F32),
            pltpu.VMEM((HEADS, T, T), F32),
            pltpu.VMEM((HEADS, T, T), F32),
            pltpu.VMEM((3, T, T), F32),
            pltpu.VMEM((HEADS, T, 128), BF16),
            pltpu.VMEM((HEADS, 128, T), BF16),
            pltpu.VMEM((HEADS, T, 256), BF16),
            pltpu.VMEM((HEADS, T, 128), BF16),
            pltpu.VMEM((HEADS, T, 128), F32),
            pltpu.VMEM((HEADS, 2, 128, 128), BF16),
            pltpu.VMEM((SLAB, 2, 128, 128), BF16),
            pltpu.VMEM((4, 128, 256), F32),
            pltpu.VMEM((SLAB, 128, 256), BF16),
            pltpu.VMEM((SLAB, 128, 128), F32),
            pltpu.VMEM((3, 128, 256), F32),
            pltpu.VMEM((2, 128, 128), BF16),
            pltpu.VMEM((ZN, 2, 128, 128), BF16),
            pltpu.VMEM((128, 128), F32),
            pltpu.VMEM((SLAB, 128, 128), BF16),
            pltpu.VMEM((SLAB, 128, 128), BF16),
            dma((4,)), dma((4,)), dma((4,)),
            dma((SLAB,)), dma((SLAB,)), dma((ZN,)), dma((ZN,)), dma((SLAB,)), dma((SLAB,)),
        ],
        compiler_params=pltpu.CompilerParams(collective_id=0, has_side_effects=True),
    )(
        doc_start,
        decay_bias,
        decay_logit.T, beta_logit.T, norm_gain[None, :],
        queries, key_input, value_input, gate_input,
    )


def solution(mesh):
    rows = P(("context", "head"), None)
    return jax.shard_map(
        body,
        mesh=mesh,
        in_specs=(rows, rows, rows, rows, rows, rows, P("head"), P(), P("context")),
        out_specs=rows,
        check_vma=False,
    )
```
